32 devices in a mesh: rep: 8 (over y, x, core), grp: 4 (over z).
Axes of the slice: x: 2, y: 2, z: 4, core: 2. Of those that a mesh axis runs over, the one named last changes fastest.
Arguments:
- tokens: bfloat16 [20480, 1024], P(('rep', 'grp')), may hold values from -6 to 6
- counts: int32 [128], P(('rep', 'grp')), may hold values from 0 to 96
- first_gain: bfloat16 [1024], P('grp'), may hold values from 0.099609375 to 1.8984375
- first_shift: bfloat16 [1024], P('grp'), may hold values from -3 to 3
- triple_weight: bfloat16 [1024, 3072], P('grp'), may hold values from -0.1875 to 0.1875
- triple_bias: bfloat16 [2048], P('grp'), may hold values from -3 to 3
- merge_weight: bfloat16 [1024, 1024], P('grp'), may hold values from -2 to 2
- merge_bias: bfloat16 [1024], P('grp'), may hold values from -1.75 to 1.75
- second_gain: bfloat16 [1024], P('grp'), may hold values from 0.099609375 to 1.8984375
- second_shift: bfloat16 [1024], P('grp'), may hold values from -3 to 3
- expand_weight: bfloat16 [1024, 4096], P('grp'), may hold values from -0.1875 to 0.1875
- expand_bias: bfloat16 [4096], P('grp'), may hold values from -3 to 3
- reduce_weight: bfloat16 [4096, 1024], P('grp'), may hold values from -0.09375 to 0.09375
- reduce_bias: bfloat16 [1024], P('grp'), may hold values from -1.75 to 1.75
- upstream: bfloat16 [20480, 1024], P(('rep', 'grp')), may hold values from -6 to 6
Outputs:
- result: bfloat16 [20480, 1024], P(('rep', 'grp'))
- tokens_slope: bfloat16 [20480, 1024], P(('rep', 'grp'))
- firstgain_slope: float32 [1024], P('grp')
- firstshift_slope: float32 [1024], P('grp')
- triple_slope: float32 [1024, 3072], P('grp')
- triplebias_slope: float32 [2048], P('grp')
- merge_slope: float32 [1024, 1024], P('grp')
- mergebias_slope: float32 [1024], P('grp')
- secondgain_slope: float32 [1024], P('grp')
- secondshift_slope: float32 [1024], P('grp')
- expand_slope: float32 [1024, 4096], P('grp')
- expandbias_slope: float32 [4096], P('grp')
- reduce_slope: float32 [4096, 1024], P('grp')
- reducebias_slope: float32 [1024], P('grp')
The draws below stay inside these ranges and needn't reach their ends.
All inputs are finite; a program needn't handle non-finite values.
Results may differ from the reference program's by a relative error of at most 0.018.
Values may be sent and summed in bfloat16 or wider, within the bound.
No kernel may reach another device: no remote copies, remote signals or barrier semaphores. Data moves between devices by JAX's collectives and lax.ppermute only.
A program may use at most 192 MiB of HBM per device.

```python
import jax
import jax.numpy as jnp
from jax import lax

D = 1024
HEADS = 16
HEAD_DIM = 64
FF = 4096
BUF = 64
KEEP = 96
SEQ_DEV = 4
SLOTS = 160
SEQS = 128
TOKENS = 20480


def plant(drawn, rng, low, largest):
    longest = drawn.shape.index(max(drawn.shape))
    spots = []
    for shift in (0, 1):
        where = [jax.random.randint(jax.random.fold_in(rng, axis), (), 0, length) for axis, length in enumerate(drawn.shape)]
        where[longest] = (where[longest] + shift) % drawn.shape[longest]
        spots.append(tuple(where))
    return drawn.at[spots[0]].set(low).at[spots[1]].set(largest)


def with_spikes(drawn, own_key, source, target, parts, factor):
    def block_of(dim):
        return (jnp.arange(drawn.shape[dim]) // (drawn.shape[dim] // parts)).reshape((-1,) + (1,) * (drawn.ndim - 1 - dim))

    near = jax.random.permutation(own_key, parts)[block_of(target)]
    other_side = (block_of(target) + parts // 2) % parts
    return jnp.where((block_of(source) == near) | (block_of(source) == other_side), factor * drawn, drawn)


def levels(rng, shape, cuts, least, top_value):
    level, own = 1.0, jax.random.fold_in(rng, 6)
    for axis_at, shards_of in cuts:
        heights = jnp.exp(jax.random.uniform(jax.random.fold_in(own, axis_at), (shards_of,), jnp.float32, least / len(cuts), top_value / len(cuts)))
        level = level * jnp.repeat(heights, shape[axis_at] // shards_of).reshape([-1 if axis == axis_at else 1 for axis in range(len(shape))])
    return level


def scatter_about(stream_key, extent, scale, limit, cuts=(), kind=jnp.bfloat16):
    factor_of = levels(stream_key, extent, cuts, -0.22, 0.18) if cuts else 1.0
    drawn = jax.random.normal(stream_key, extent, jnp.float32) * scale * factor_of
    return jnp.minimum(jnp.maximum(drawn, -limit), limit).astype(kind)


def heavy_noise(own_key, shape, scale, limit, shards, heavy, kind=jnp.bfloat16):
    result = scale * jax.random.normal(own_key, shape, jnp.float32)
    if shards:
        result = result * levels(own_key, shape, shards, -0.22, 0.18)
    return jnp.clip(with_spikes(result, jax.random.fold_in(own_key, 3), *heavy), -limit, limit).astype(kind)


def setup_inputs(seed: int = 0) -> dict:
    seeds = jax.random.split(jax.random.key(seed), 16)
    tokens = heavy_noise(seeds[0], (TOKENS, D), 1.0, 6.0, ((0, 32),), (0, 1, 32, 2.75))
    counts = plant(jax.random.randint(seeds[1], (SEQS,), 0, KEEP + 1), jax.random.fold_in(seeds[1], 1), 0, KEEP).astype(jnp.int32)
    first_gain = jnp.clip(1.0 + 0.18 * jax.random.normal(seeds[2], (D,), jnp.float32), 0.099609375, 1.8984375).astype(jnp.bfloat16)
    first_shift = scatter_about(seeds[3], (D,), 0.5, 3.0, ((0, 4),))
    triple_weight = scatter_about(seeds[4], (D, 3 * D), D ** -0.5, 0.1875, ((0, 4),))
    triple_bias = scatter_about(seeds[5], (2 * D,), 0.5, 3.0, ((0, 4),))
    merge_weight = scatter_about(seeds[6], (D, D), (max(D // 128, 1)) ** -0.5, 2.0, ((0, 4),))
    merge_bias = scatter_about(seeds[7], (D,), 0.3, 1.75, ((0, 4),))
    second_gain = jnp.clip(1.0 + 0.18 * jax.random.normal(seeds[8], (D,), jnp.float32), 0.099609375, 1.8984375).astype(jnp.bfloat16)
    second_shift = scatter_about(seeds[9], (D,), 0.5, 3.0, ((0, 4),))
    expand_weight = scatter_about(seeds[10], (D, FF), D ** -0.5, 0.1875, ((0, 4),))
    expand_bias = scatter_about(seeds[11], (FF,), 0.5, 3.0, ((0, 4),))
    reduce_weight = scatter_about(seeds[12], (FF, D), FF ** -0.5, 0.09375, ((0, 4),))
    reduce_bias = scatter_about(seeds[13], (D,), 0.3, 1.75, ((0, 4),))
    upstream = scatter_about(seeds[14], (TOKENS, D), 1.0, 6.0, ((0, 32),))
    return dict(tokens=tokens, counts=counts, first_gain=first_gain, first_shift=first_shift, triple_weight=triple_weight, triple_bias=triple_bias, merge_weight=merge_weight, merge_bias=merge_bias, second_gain=second_gain, second_shift=second_shift, expand_weight=expand_weight, expand_bias=expand_bias, reduce_weight=reduce_weight, reduce_bias=reduce_bias, upstream=upstream)


@jax.custom_vjp
def low(v):
    return lax.optimization_barrier(v.astype(jnp.bfloat16)).astype(jnp.float32)

@jax.custom_vjp
def low_back(v):
    return v

def low_keep(v):
    return (low(v), None)

def low_pass(kept, grad):
    return (grad,)

def back_keep(v):
    return (v, None)

def back_low(kept, grad):
    return (low(grad),)
low.defvjp(low_keep, low_pass)
low_back.defvjp(back_keep, back_low)

def layer_norm(values, gain, shift):
    center = values - lax.optimization_barrier(jnp.mean(values, axis=-1, keepdims=True))
    spread = lax.optimization_barrier(jnp.mean(center * center, axis=-1, keepdims=True))
    return center * lax.rsqrt(spread + 1e-06) * gain + shift

def layer_block(params, block_tokens, block_counts):
    gain_one, shift_one, triple_w, triple_b, merge_w, merge_b, gain_two, shift_two, expand_w, expand_b, reduce_w, reduce_b = params
    high = lax.Precision.HIGHEST
    groups = block_counts.shape[0]
    slot_index = lax.broadcasted_iota(jnp.int32, (groups, SLOTS), 1)
    live = (slot_index < BUF + block_counts[:, None]).astype(jnp.float32)
    normed = low(layer_norm(block_tokens, gain_one, shift_one))
    bias_full = jnp.concatenate([triple_b[:D], jnp.zeros((D,), jnp.float32), triple_b[D:]])
    triple = low_back(low(jnp.einsum('gld,de->gle', normed, triple_w, precision=high) + bias_full))
    query = triple[..., :D].reshape(groups, SLOTS, HEADS, HEAD_DIM)
    keys = triple[..., D:2 * D].reshape(groups, SLOTS, HEADS, HEAD_DIM)
    values = triple[..., 2 * D:].reshape(groups, SLOTS, HEADS, HEAD_DIM)
    scores = low_back(jnp.einsum('gqhd,gkhd->ghqk', query, keys, precision=high)) * HEAD_DIM ** (-0.5)
    scores = jnp.where(live[:, None, None, :] > 0, scores, -1e+30)
    weights = low(jax.nn.softmax(scores, axis=-1))
    attended = jnp.einsum('ghqk,gkhd->gqhd', weights, values, precision=high)
    attended = low_back(low(attended)).reshape(groups, SLOTS, D)
    branch = low_back(jnp.einsum('gla,ad->gld', attended, merge_w, precision=high) + merge_b)
    resid = block_tokens + branch
    normed_two = low(layer_norm(resid, gain_two, shift_two))
    pre_act = low_back(jnp.einsum('gld,df->glf', normed_two, expand_w, precision=high) + expand_b)
    hidden = low(jax.nn.gelu(pre_act, approximate=False))
    reduced = low_back(jnp.einsum('glf,fd->gld', hidden, reduce_w, precision=high) + reduce_b)
    return (resid + reduced) * live[..., None]

def reference(tokens, counts, first_gain, first_shift, triple_weight, triple_bias, merge_weight, merge_bias, second_gain, second_shift, expand_weight, expand_bias, reduce_weight, reduce_bias, upstream):
    params = (first_gain, first_shift, triple_weight, triple_bias, merge_weight, merge_bias, second_gain, second_shift, expand_weight, expand_bias, reduce_weight, reduce_bias)
    params = tuple((item.astype(jnp.float32) for item in params))
    block = SEQ_DEV * 4
    blocks = SEQS // block
    checked = jax.checkpoint(layer_block)

    def forward(tokens_f, params_f):
        token_blocks = tokens_f.reshape(blocks, block, SLOTS, D)
        count_blocks = counts.reshape(blocks, block)
        outcome = lax.map(lambda pair: checked(params_f, pair[0], pair[1]), (token_blocks, count_blocks))
        return outcome.reshape(TOKENS, D)
    outcome, backward = jax.vjp(forward, tokens.astype(jnp.float32), params)
    token_grad, param_grad = backward(upstream.astype(jnp.float32))
    g_one, s_one, t_w, t_b, m_w, m_b, g_two, s_two, e_w, e_b, r_w, r_b = param_grad
    return (outcome.astype(jnp.bfloat16), token_grad.astype(jnp.bfloat16), g_one, s_one, t_w, t_b, m_w, m_b, g_two, s_two, e_w, e_b, r_w, r_b)
```

```python
import functools
import math

import jax
import jax.numpy as jnp
from jax import lax
from jax.experimental import pallas as pl
from jax.experimental.pallas import tpu as pltpu
from jax.sharding import PartitionSpec as P

HEADS = 16
BUF = 64


F32 = jnp.float32
LOW = jnp.bfloat16
CORE, ACROSS, UP = 1, 2, 4
VEC = ("first_gain", "first_shift", "triple_bias", "merge_bias", "second_gain", "second_shift", "expand_bias", "reduce_bias")


def whole(shape):
    zeros = (0,) * len(shape)
    return pl.BlockSpec(shape, lambda *_: zeros)


def dot(a, b):
    return jnp.dot(a, b, preferred_element_type=F32)


def dot_nt(a, b):
    return lax.dot_general(a, b, (((1,), (1,)), ((), ())), preferred_element_type=F32)


def dot_tn(a, b):
    return lax.dot_general(a, b, (((0,), (0,)), ((), ())), preferred_element_type=F32)


def at(start, size):
    return pl.ds(pl.multiple_of(start, size), size)


def norm_parts(values):
    center = values - jnp.mean(values, axis=-1, keepdims=True)
    rstd = lax.rsqrt(jnp.mean(center * center, axis=-1, keepdims=True) + 1e-06)
    return center * rstd, rstd


def norm_grad(hat, rstd, gain, grad):
    scaled = grad * gain
    mean = jnp.mean(scaled, axis=-1, keepdims=True)
    along = jnp.mean(scaled * hat, axis=-1, keepdims=True)
    return rstd * (scaled - mean - hat * along)


def normal_parts(u):
    bell = jnp.exp(u * u * -0.5)
    t = 1.0 / (1.0 + jnp.abs(u) * (0.3275911 / math.sqrt(2.0)))
    poly = ((((1.061405429 * t - 1.453152027) * t + 1.421413741) * t - 0.284496736) * t + 0.254829592) * t
    tail = 0.5 * poly * bell
    return jnp.where(u < 0, tail, 1.0 - tail), bell


def place(step, me, parts, put):
    me_k, me_z = me[1], me[2]
    m, x1, y1, x2, y2 = parts[:5]
    mc, x1c, y1c, x2c, y2c = parts[5:]
    for number, pieces in enumerate((((m, mc, 0),), ((x1, x1c, 0),), ((y1, y1c, 0),), ((x2, x2c, 0), (y2, y2c, 64)))):

        @pl.when(step == number)
        def _(pieces=pieces):
            for mine, other, row in pieces:
                for s in (1, 2, 3):
                    z = lax.rem(me_z + 4 - s, 4)
                    put(me_k, z, row, mine.at[s - 1])
                    put(1 - me_k, z, row, other.at[s - 1])


def attend_kernel(me, counts, tokens, gain, shift, bias, t0, t1, t2, g0, *rest):
    parts, (first, qkv, att, full) = rest[:10], rest[10:]
    step = pl.program_id(0)
    slots = tokens.shape[0] // 4

    @pl.when(step == 0)
    def _():
        for s in range(4):
            rows = pl.ds(s * slots, slots)
            hat, _ = norm_parts(tokens[rows, :].astype(F32))
            first[rows, :] = (hat * gain[...] + shift[...]).astype(LOW)

    def put(k, z, row, ref):
        n = ref.shape[0]
        full[0, pl.ds(pl.multiple_of(z * 256 + k * 128 + row, 64), n), :] = ref[...]

    place(step, me, parts, put)
    for t, own in enumerate((t0, t1, t2, g0)):
        full[0, at(me[2] * 256, 256), t * 256 : (t + 1) * 256] = own[...]
    qkv[0] = (dot(first[...], full[0, :, :768]) + bias[0]).astype(LOW)
    lanes = lax.broadcasted_iota(jnp.int32, (1, 128), 1)
    halves = ((lanes < 64).astype(LOW), (lanes >= 64).astype(LOW))
    keys_at = lax.broadcasted_iota(jnp.int32, (1, slots), 1)

    def sequence(s, carry):
        rows = pl.ds(pl.multiple_of(s * slots, 32), slots)
        live = keys_at < BUF + counts[s]
        for pair in range(2):
            q = qkv[0, rows, pair * 128 : pair * 128 + 128]
            k = qkv[0, rows, 256 + pair * 128 : 384 + pair * 128]
            v = qkv[0, rows, 512 + pair * 128 : 640 + pair * 128]
            total = None
            for half in halves:
                scores = jnp.where(live, dot_nt(q * half, k) * 0.125, -1e30)
                e = jnp.exp(scores - jnp.max(scores, axis=-1, keepdims=True))
                probs = e * (1.0 / jnp.sum(e, axis=-1, keepdims=True))
                out = dot(probs.astype(LOW), v * half)
                total = out if total is None else total + out
            att[rows, pair * 128 : pair * 128 + 128] = total.astype(LOW)
        return carry

    lax.fori_loop(0, 4, sequence, 0)


def merge_kernel(me, att, wm, tokens, bias, gain, shift, resid, second):
    step = pl.program_id(0)
    cols = at((me[0] ^ step) * 256, 256)
    resid[:, cols] = tokens[:, cols].astype(F32) + (dot(att[...], wm[0]) + bias[:, cols])

    @pl.when(step == 3)
    def _():
        n = resid.shape[0] // 4
        for s in range(4):
            rows = pl.ds(s * n, n)
            hat, _ = norm_parts(resid[rows, :])
            second[rows, :] = (hat * gain[...] + shift[...]).astype(LOW)


def scatter_out(me, keep, send, zk, cols, values):
    s = lax.rem(me[2] * 3 + 4 + zk // 2, 4)
    mine = me[1] == zk % 2

    @pl.when(mine)
    def _():
        keep[0, s, :, cols] = values

    @pl.when(jnp.logical_not(mine))
    def _():
        send[0, s, :, cols] = values


def feed_kernel(me, second, g_out, e0, e1, e2, e3, r0, bias, *rest):
    parts, (keep, send, db, reduced, g_second, ew, rw, de, dr) = rest[:10], rest[10:]
    step = pl.program_id(0)

    def put(k, z, row, ref):
        n = ref.shape[0]
        ew[pl.ds(pl.multiple_of(z * 256 + k * 128 + row, 64), n), :] = ref[:, :512]
        rw[pl.ds(pl.multiple_of(z * 128 + row, 64), n), at(k * 512, 512)] = ref[:, 512:]

    place(step, me, parts, put)
    for z, own in enumerate((e0, e1, e2, e3)):
        ew[at(me[2] * 256, 256), z * 128 : z * 128 + 128] = own[...]
    rw[at(me[2] * 128, 128), :] = r0[...]
    s = second[...]
    g = g_out[...]
    for j in range(2):
        cols = slice(j * 256, j * 256 + 256)
        e, r = ew[:, cols], rw[cols, :]
        pre = dot(s, e) + bias[0, :, cols]
        g_hidden = dot_nt(g, r)
        phi, bell = normal_parts(pre)
        hidden = (pre * phi).astype(LOW)
        g_pre = (g_hidden * (phi + pre * bell * (1.0 / math.sqrt(2.0 * math.pi)))).astype(LOW)
        de[:, cols] = dot_tn(s, g_pre).astype(LOW)
        dr[cols, :] = dot_tn(hidden, g).astype(LOW)
        db[0, :, cols] = jnp.sum(g_pre.astype(F32), axis=0, keepdims=True)
        more, g_more = dot(hidden, r), dot_nt(g_pre, e)
        if j == 0:

            @pl.when(step == 0)
            def _():
                reduced[...] = more
                g_second[...] = g_more

            @pl.when(step > 0)
            def _():
                reduced[...] += more
                g_second[...] += g_more
        else:
            reduced[...] += more
            g_second[...] += g_more
    for zk in range(8):
        z, k = zk // 2, zk % 2
        scatter_out(me, keep, send, zk, slice(0, 512), de[zk * 128 : zk * 128 + 128, :])
        scatter_out(me, keep, send, zk, slice(512, 1024), dr[z * 128 : z * 128 + 128, k * 512 : k * 512 + 512])


def turn_kernel(me, counts, resid, red0, red1, gs0, gs1, upstream, bias, gain, wm, result, g_resid, g_branch, g_att, sums, acc):
    step = pl.program_id(0)
    n = resid.shape[0] // 4

    @pl.when(step == 0)
    def _():
        sums[...] = jnp.zeros_like(sums)
        slot = lax.broadcasted_iota(jnp.int32, (n, 1), 0)
        for s in range(4):
            rows = pl.ds(s * n, n)
            live = (slot < BUF + counts[s]).astype(F32)
            x = resid[rows, :]
            result[rows, :] = ((x + (red0[rows, :] + red1[rows, :] + bias[...])) * live).astype(LOW)
            up = upstream[rows, :].astype(F32) * live
            hat, rstd = norm_parts(x)
            grad = gs0[rows, :] + gs1[rows, :]
            total = up + norm_grad(hat, rstd, gain[...], grad)
            g_resid[rows, :] = total
            low = total.astype(LOW)
            g_branch[rows, :] = low
            sums[0:1, :] += jnp.sum(grad * hat, axis=0, keepdims=True)
            sums[1:2, :] += jnp.sum(grad, axis=0, keepdims=True)
            sums[2:3, :] += jnp.sum(low.astype(F32), axis=0, keepdims=True)
            sums[3:4, :] += jnp.sum(up.astype(LOW).astype(F32), axis=0, keepdims=True)

    more = dot_nt(g_branch[:, at((me[0] ^ step) * 256, 256)], wm[0])

    @pl.when(step == 0)
    def _():
        acc[...] = more

    @pl.when(step > 0)
    def _():
        acc[...] += more

    @pl.when(step == 3)
    def _():
        g_att[...] = acc[...].astype(LOW)


def attend_back_kernel(me, counts, qkv, g_att, first, att, g_branch, full, keep, send, db, g_first, dq):
    step = pl.program_id(0)
    slots = first.shape[0] // 4
    lanes = lax.broadcasted_iota(jnp.int32, (1, 128), 1)
    halves = ((lanes < 64).astype(LOW), (lanes >= 64).astype(LOW))
    keys_at = lax.broadcasted_iota(jnp.int32, (slots, 1), 0)

    def sequence(s, carry):
        rows = pl.ds(pl.multiple_of(s * slots, 32), slots)
        live = keys_at < BUF + counts[s]
        for pair in range(2):
            q = qkv[0, rows, pair * 128 : pair * 128 + 128]
            k = qkv[0, rows, 256 + pair * 128 : 384 + pair * 128]
            v = qkv[0, rows, 512 + pair * 128 : 640 + pair * 128]
            g = g_att[rows, pair * 128 : pair * 128 + 128]
            g_q = g_k = g_v = 0.0
            for half in halves:
                q_h, g_h = q * half, g * half
                scores = jnp.where(live, dot_nt(k, q_h) * 0.125, -1e30)
                e = jnp.exp(scores - jnp.max(scores, axis=0, keepdims=True))
                probs = e * (1.0 / jnp.sum(e, axis=0, keepdims=True))
                g_probs = dot_nt(v, g_h)
                inner = jnp.sum(probs * g_probs, axis=0, keepdims=True)
                g_scores = (probs * (g_probs - inner) * 0.125).astype(LOW)
                g_v += dot(probs.astype(LOW), g_h)
                g_k += dot(g_scores, q_h)
                g_q += dot_tn(g_scores, k * half)
            dq[rows, pair * 128 : pair * 128 + 128] = g_q.astype(LOW)
            dq[rows, 256 + pair * 128 : 384 + pair * 128] = g_k.astype(LOW)
            dq[rows, 512 + pair * 128 : 640 + pair * 128] = g_v.astype(LOW)
        return carry

    lax.fori_loop(0, 4, sequence, 0)
    db[0, :, 0:256] = jnp.sum(dq[:, 0:256].astype(F32), axis=0, keepdims=True)
    db[0, :, 256:512] = jnp.sum(dq[:, 512:768].astype(F32), axis=0, keepdims=True)
    more = dot_nt(dq[...], full[0, :, :768])

    @pl.when(step == 0)
    def _():
        g_first[...] = more

    @pl.when(step > 0)
    def _():
        g_first[...] += more

    for t in range(4):
        cols = slice(t * 256, t * 256 + 256)
        if t < 3:
            piece = dot_tn(first[...], dq[:, cols]).astype(LOW)
        else:
            piece = dot_tn(att[...], g_branch[:, at((me[0] ^ step) * 256, 256)]).astype(LOW)
        for zk in range(8):
            scatter_out(me, keep, send, zk, cols, piece[zk * 128 : zk * 128 + 128, :])


def last_kernel(tokens, g_first, g_resid, gain, slope, sums):
    n = tokens.shape[0] // 4
    sums[...] = jnp.zeros_like(sums)
    for s in range(4):
        rows = pl.ds(s * n, n)
        hat, rstd = norm_parts(tokens[rows, :].astype(F32))
        grad = g_first[rows, :]
        slope[rows, :] = (g_resid[rows, :] + norm_grad(hat, rstd, gain[...], grad)).astype(LOW)
        sums[0:1, :] += jnp.sum(grad * hat, axis=0, keepdims=True)
        sums[1:2, :] += jnp.sum(grad, axis=0, keepdims=True)


def owned_attend_kernel(me, *refs):
    parts, (triple, merge) = refs[:10], refs[10:]
    for j in range(4):
        p = me[0] ^ j
        for other in range(2):
            k = me[1] ^ other
            mine = parts[other * 5 : other * 5 + 5]
            blocks = ((mine[j], 0, 128),) if j < 3 else ((mine[3], 0, 64), (mine[4], 64, 64))
            for block, row, n in blocks:
                rows = pl.ds(pl.multiple_of(k * 128 + row, 64), n)
                for t in range(3):
                    triple[rows, at(t * 1024 + p * 256, 256)] = block[:, t * 256 : t * 256 + 256].astype(F32)
                merge[rows, at(p * 256, 256)] = block[:, 768:].astype(F32)


def owned_feed_kernel(me, *refs):
    parts, (expand, reduce) = refs[:10], refs[10:]
    for j in range(4):
        p = me[0] ^ j
        for c in range(2):
            place_at = c * 4 + p
            for other in range(2):
                k = me[1] ^ other
                ref = parts[other * 5 + (j if j < 3 else 3 + c)]
                values = ref[c if j < 3 else 0]
                rows = at(k * 128, 128)
                for z in range(4):
                    expand[rows, at(z * 1024 + place_at * 128, 128)] = values[:, z * 128 : z * 128 + 128].astype(F32)
                reduce[at(place_at * 128, 128), at(k * 512, 512)] = values[:, 512:].astype(F32)


def swap(values, bit):
    return lax.ppermute(values, "rep", [(r, r ^ bit) for r in range(8)])


def shift_plane(values, s):
    return lax.ppermute(values, "grp", [(z, (z + s) % 4) for z in range(4)])


def share_plane(mine, axis):
    half = mine.shape[axis] // 2
    x1, y1 = swap(mine, ACROSS), swap(mine, UP)
    x2 = swap(lax.slice_in_dim(x1, 0, half, axis=axis), UP)
    y2 = swap(lax.slice_in_dim(y1, half, 2 * half, axis=axis), ACROSS)
    got = (mine, x1, y1, x2, y2)
    return got + tuple(swap(value, CORE) for value in got)


def low_sum(*terms):
    total = terms[0].astype(F32)
    for term in terms[1:]:
        total = total + term.astype(F32)
    return total.astype(LOW)


def sum_to_owner(keep, send):
    got = swap(send, CORE)
    d_a = swap(low_sum(keep[3, :2], got[3, :2]), ACROSS)
    d_b = swap(low_sum(keep[3, 2:], got[3, 2:]), UP)
    x_a, x_b = low_sum(keep[1, :2], got[1, :2]), low_sum(keep[1, 2:], got[1, 2:], d_b)
    y_a, y_b = low_sum(keep[2, :2], got[2, :2], d_a), low_sum(keep[2, 2:], got[2, 2:])
    x = swap(jnp.concatenate([x_a, x_b]), ACROSS)
    y = swap(jnp.concatenate([y_a, y_b]), UP)
    mine = [low_sum(keep[0, s], got[0, s], x[s], y[s]) for s in range(4)]
    return low_sum(mine[0], *(shift_plane(mine[s], s) for s in (1, 2, 3)))


def by_plane(stacked, me_z):
    return lax.dynamic_slice_in_dim(jnp.concatenate([stacked, stacked]), lax.rem(4 - me_z, 4), 4)


def from_plane(stacked, me_z):
    return lax.dynamic_slice_in_dim(jnp.concatenate([stacked, stacked]), me_z, 4)


def fast_device(
    tokens, counts, first_gain, first_shift, triple_weight, triple_bias, merge_weight, merge_bias,
    second_gain, second_shift, expand_weight, expand_bias, reduce_weight, reduce_bias, upstream,
):
    rows, width = tokens.shape
    slots = rows // 4
    me_r, me_z = lax.axis_index("rep"), lax.axis_index("grp")
    me_p, me_k = me_r // 2, me_r % 2
    me = jnp.stack([me_p, me_k, me_z]).astype(jnp.int32)

    d_rows = lax.dynamic_slice_in_dim
    half_t = d_rows(triple_weight, me_k * 128, 128)
    half_m = d_rows(merge_weight, me_k * 128, 128)
    mine_a = jnp.concatenate([d_rows(half_t, t * 1024 + me_p * 256, 256, axis=1) for t in range(3)] + [d_rows(half_m, me_p * 256, 256, axis=1)], axis=1)
    half_e = d_rows(expand_weight, me_k * 128, 128)
    half_r = d_rows(reduce_weight, me_k * 512, 512, axis=1)
    mine_f = [
        jnp.concatenate(
            [d_rows(half_e, z * 1024 + (c * 4 + me_p) * 128, 128, axis=1) for z in range(4)] + [d_rows(half_r, (c * 4 + me_p) * 128, 128)],
            axis=1,
        )
        for c in range(2)
    ]
    vec = jnp.concatenate([first_gain, first_shift, triple_bias, merge_bias, second_gain, second_shift, expand_bias, reduce_bias])
    pad = jnp.zeros((13, 1024), LOW)
    sent_a = jnp.concatenate([mine_a, vec.reshape(3, 1024), pad])
    got_a = [shift_plane(sent_a, s) for s in (1, 2, 3)]
    got_f = [jnp.stack([shift_plane(m, s) for s in (1, 2, 3)]) for m in mine_f]
    parts_a = share_plane(jnp.stack([g[:128] for g in got_a]), 1)
    parts_f = [share_plane(g, 1) for g in got_f]

    ahead = jnp.stack([vec.reshape(3072)] + [got_a[s - 1][128:131].reshape(3072) for s in (3, 2, 1)])
    vecs = by_plane(ahead, me_z).astype(F32)
    sizes = (256, 256, 512, 256, 256, 256, 1024, 256)
    whole_vec, begin = {}, 0
    for name, size in zip(VEC, sizes):
        whole_vec[name] = vecs[:, begin : begin + size].reshape(1, 4 * size)
        begin += size
    q_bias, v_bias = whole_vec["triple_bias"][0, :1024].reshape(4, 256), whole_vec["triple_bias"][0, 1024:].reshape(4, 256)
    bias_a = jnp.concatenate([q_bias, jnp.zeros((4, 256), F32), v_bias], axis=1).reshape(4, 1, 768)
    bias_f = whole_vec["expand_bias"].reshape(4, 8, 128).transpose(1, 0, 2).reshape(8, 1, 512)

    live = (lax.broadcasted_iota(jnp.int32, (4, slots), 1) < BUF + counts[:, None]).astype(F32).reshape(rows, 1)
    g_out = (upstream.astype(F32) * live).astype(LOW)

    sds = jax.ShapeDtypeStruct

    def call(body, prefetch, grid, in_specs, out_specs, out_shape, scratch, flops, moved, name):
        spec = pltpu.PrefetchScalarGridSpec(num_scalar_prefetch=prefetch, grid=grid, in_specs=in_specs, out_specs=out_specs, scratch_shapes=scratch)
        return pl.pallas_call(
            body, grid_spec=spec, out_shape=out_shape, name=name,
            cost_estimate=pl.CostEstimate(flops=flops, bytes_accessed=moved, transcendentals=0),
        )

    full_rows = whole((rows, width))
    row = whole((1, width))

    def chip(step, me):
        return me[0] ^ step

    part_specs = [whole((3, 128, 1024))] * 3 + [whole((3, 64, 1024))] * 2
    part_specs = part_specs * 2

    first, qkv, att, full = call(
        attend_kernel, 2, (4,),
        [full_rows, row, row, pl.BlockSpec((1, 1, 768), lambda i, me, n: (chip(i, me), 0, 0))]
        + [pl.BlockSpec((256, 256), lambda i, me, n, t=t: (0, t * 4 + chip(i, me))) for t in range(3)]
        + [pl.BlockSpec((256, 256), lambda i, me, n: (0, chip(i, me)))]
        + part_specs,
        [
            full_rows,
            pl.BlockSpec((1, rows, 768), lambda i, me, n: (i, 0, 0)),
            pl.BlockSpec((rows, 256), lambda i, me, n: (0, chip(i, me))),
            pl.BlockSpec((1, 1024, 1024), lambda i, me, n: (i, 0, 0)),
        ],
        [sds((rows, width), LOW), sds((4, rows, 768), LOW), sds((rows, width), LOW), sds((4, 1024, 1024), LOW)],
        [], 8_000_000_000, 30_000_000, "attend",
    )(me, counts, tokens, whole_vec["first_gain"], whole_vec["first_shift"], bias_a, triple_weight, triple_weight, triple_weight, merge_weight, *parts_a)

    wm_spec = pl.BlockSpec((1, 1024, 256), lambda i, *_: (i, 0, 3))
    resid, second = call(
        merge_kernel, 1, (4,), [full_rows, wm_spec, full_rows, row, row, row], [full_rows, full_rows],
        [sds((rows, width), F32), sds((rows, width), LOW)], [], 1_400_000_000, 9_000_000, "merge",
    )(me, att, full, tokens, whole_vec["merge_bias"], whole_vec["second_gain"], whole_vec["second_shift"])

    grad_spec = pl.BlockSpec((1, 4, 128, 1024), lambda i, *_: (i, 0, 0, 0))
    grad_shape = sds((4, 4, 128, 1024), LOW)
    outs_f = []
    for c in range(2):
        outs_f.append(
            call(
                feed_kernel, 1, (4,),
                [full_rows, full_rows]
                + [pl.BlockSpec((256, 128), lambda i, me, z=z, c=c: (0, z * 8 + c * 4 + chip(i, me))) for z in range(4)]
                + [pl.BlockSpec((128, 1024), lambda i, me, c=c: (c * 4 + chip(i, me), 0))]
                + [pl.BlockSpec((1, 1, 512), lambda i, me, c=c: (c * 4 + chip(i, me), 0, 0))]
                + part_specs,
                [grad_spec, grad_spec, pl.BlockSpec((1, 1, 512), lambda i, me: (chip(i, me), 0, 0)), full_rows, full_rows],
                [grad_shape, grad_shape, sds((4, 1, 512), F32), sds((rows, width), F32), sds((rows, width), F32)],
                [pltpu.VMEM((1024, 512), LOW), pltpu.VMEM((512, 1024), LOW), pltpu.VMEM((1024, 512), LOW), pltpu.VMEM((512, 1024), LOW)],
                16_000_000_000, 30_000_000, "feed",
            )(me, second, g_out, *([expand_weight] * 4), reduce_weight, bias_f, *parts_f[c])
        )
    owned_f = [sum_to_owner(o[0], o[1]) for o in outs_f]
    parts = share_plane(jnp.stack(owned_f), 0)
    expand_slope, reduce_slope = call(
        owned_feed_kernel, 1, (1,), [whole(p.shape) for p in parts], [whole((256, 4096)), whole((1024, 1024))],
        [sds((256, 4096), F32), sds((1024, 1024), F32)], [], 1_000_000, 12_000_000, "owned_feed",
    )(me, *parts)

    result, g_resid, g_branch, g_att, sums_two = call(
        turn_kernel, 2, (4,), [full_rows] * 6 + [row, row, wm_spec],
        [full_rows, full_rows, full_rows, full_rows, whole((8, width))],
        [sds((rows, width), LOW), sds((rows, width), F32), sds((rows, width), LOW), sds((rows, width), LOW), sds((8, width), F32)],
        [pltpu.VMEM((rows, width), F32)], 1_400_000_000, 25_000_000, "turn",
    )(me, counts, resid, outs_f[0][3], outs_f[1][3], outs_f[0][4], outs_f[1][4], upstream, whole_vec["reduce_bias"], whole_vec["second_gain"], full)

    keep_a, send_a, db_a, g_first = call(
        attend_back_kernel, 2, (4,),
        [
            pl.BlockSpec((1, rows, 768), lambda i, *_: (i, 0, 0)),
            pl.BlockSpec((rows, 256), lambda i, me, n: (0, chip(i, me))),
            full_rows, full_rows, full_rows,
            pl.BlockSpec((1, 1024, 1024), lambda i, *_: (i, 0, 0)),
        ],
        [grad_spec, grad_spec, pl.BlockSpec((1, 1, 512), lambda i, me, n: (chip(i, me), 0, 0)), full_rows],
        [grad_shape, grad_shape, sds((4, 1, 512), F32), sds((rows, width), F32)],
        [pltpu.VMEM((rows, 768), LOW)], 16_000_000_000, 30_000_000, "attend_back",
    )(me, counts, qkv, g_att, first, att, g_branch, full)
    owned_a = sum_to_owner(keep_a, send_a)
    parts = share_plane(owned_a, 0)
    triple_slope, merge_slope = call(
        owned_attend_kernel, 1, (1,), [whole(p.shape) for p in parts], [whole((256, 3072)), whole((256, 1024))],
        [sds((256, 3072), F32), sds((256, 1024), F32)], [], 1_000_000, 6_000_000, "owned_attend",
    )(me, *parts)

    tokens_slope, sums_one = call(
        last_kernel, 0, (1,), [full_rows, full_rows, full_rows, row], [full_rows, whole((8, width))],
        [sds((rows, width), LOW), sds((8, width), F32)], [], 1_000_000, 8_000_000, "last",
    )(tokens, g_first, g_resid, whole_vec["first_gain"])

    db_f = jnp.concatenate([o[2].reshape(4, 512) for o in outs_f]).reshape(8, 4, 128).transpose(1, 0, 2).reshape(4096)
    db_qv = db_a.reshape(4, 2, 256).transpose(1, 0, 2).reshape(2048)
    grads = {
        "first_gain": sums_one[0], "first_shift": sums_one[1], "triple_bias": db_qv, "merge_bias": sums_two[2],
        "second_gain": sums_two[0], "second_shift": sums_two[1], "expand_bias": db_f, "reduce_bias": sums_two[3],
    }
    vec_grads = jnp.concatenate([grads[name].reshape(4, -1) for name in VEC], axis=1)
    vec_grads = from_plane(vec_grads, me_z)
    for bit in (CORE, ACROSS, UP):
        vec_grads = vec_grads + swap(vec_grads, bit)
    own = vec_grads[0]
    for s in (1, 2, 3):
        own = own + shift_plane(vec_grads[s], s)
    slopes, begin = {}, 0
    for name, size in zip(VEC, sizes):
        slopes[name] = own[begin : begin + size]
        begin += size
    return (
        result, tokens_slope, slopes["first_gain"], slopes["first_shift"], triple_slope, slopes["triple_bias"], merge_slope, slopes["merge_bias"],
        slopes["second_gain"], slopes["second_shift"], expand_slope, slopes["expand_bias"], reduce_slope, slopes["reduce_bias"],
    )


def layer_norm(values, gain, shift):
    center = values - jnp.mean(values, axis=-1, keepdims=True)
    spread = jnp.mean(center * center, axis=-1, keepdims=True)
    return center * lax.rsqrt(spread + 1e-06) * gain + shift


def exact_gelu(values):
    return jax.nn.gelu(values, approximate=False)


def column_sums(values):
    return jnp.sum(values.astype(jnp.float32), axis=0)


def per_device(
    tokens,
    counts,
    first_gain,
    first_shift,
    triple_weight,
    triple_bias,
    merge_weight,
    merge_bias,
    second_gain,
    second_shift,
    expand_weight,
    expand_bias,
    reduce_weight,
    reduce_bias,
    upstream,
):
    f32 = jnp.float32
    low_type = jnp.bfloat16
    groups = counts.shape[0]
    rows, width = tokens.shape
    slots = rows // groups
    heads = HEADS
    head_size = width // heads
    scale = head_size ** (-0.5)
    attend_set = (
        lax.all_gather(first_gain, "grp", axis=0, tiled=True),
        lax.all_gather(first_shift, "grp", axis=0, tiled=True),
        lax.all_gather(triple_weight, "grp", axis=0, tiled=True),
        lax.all_gather(triple_bias, "grp", axis=0, tiled=True),
        lax.all_gather(merge_weight, "grp", axis=0, tiled=True),
        lax.all_gather(merge_bias, "grp", axis=0, tiled=True),
    )
    feed_set = (
        lax.all_gather(second_gain, "grp", axis=0, tiled=True),
        lax.all_gather(second_shift, "grp", axis=0, tiled=True),
        lax.all_gather(expand_weight, "grp", axis=0, tiled=True),
        lax.all_gather(expand_bias, "grp", axis=0, tiled=True),
        lax.all_gather(reduce_weight, "grp", axis=0, tiled=True),
        lax.all_gather(reduce_bias, "grp", axis=0, tiled=True),
    )
    gain_one, shift_one, triple_full, triple_vec, merge_full, merge_vec = attend_set
    gain_two, shift_two, expand_full, expand_vec, reduce_full, reduce_vec = feed_set
    slot_index = lax.broadcasted_iota(jnp.int32, (groups, slots), 1)
    live = (slot_index < BUF + counts[:, None]).astype(f32)
    live_rows = live.reshape(rows, 1)
    key_live = live[:, None, None, :] > 0
    tokens_f = tokens.astype(f32)
    normed_one, first_back = jax.vjp(
        layer_norm, tokens_f, gain_one.astype(f32), shift_one.astype(f32)
    )
    normed_low = normed_one.astype(low_type)
    bias_vec = triple_vec.astype(f32)
    bias_full = jnp.concatenate([bias_vec[:width], jnp.zeros((width,), f32), bias_vec[width:]])
    triple = (jnp.dot(normed_low, triple_full, preferred_element_type=f32) + bias_full).astype(
        low_type
    )
    query = triple[:, :width].reshape(groups, slots, heads, head_size)
    keys = triple[:, width : 2 * width].reshape(groups, slots, heads, head_size)
    values = triple[:, 2 * width :].reshape(groups, slots, heads, head_size)

    def make_scores():
        raw = jnp.einsum("gqhd,gkhd->ghqk", query, keys, preferred_element_type=f32) * scale
        return jnp.where(key_live, raw, -1e30)

    scores = make_scores()
    top = jnp.max(scores, axis=-1, keepdims=True)
    log_total = top + jnp.log(jnp.sum(jnp.exp(scores - top), axis=-1, keepdims=True))
    weights = jnp.exp(scores - log_total)
    attended = jnp.einsum(
        "ghqk,gkhd->gqhd", weights.astype(low_type), values, preferred_element_type=f32
    )
    attended = attended.reshape(rows, width).astype(low_type)
    branch = jnp.dot(attended, merge_full, preferred_element_type=f32) + merge_vec.astype(f32)
    resid = tokens_f + branch
    normed_two, second_back = jax.vjp(
        layer_norm, resid, gain_two.astype(f32), shift_two.astype(f32)
    )
    second_low = normed_two.astype(low_type)
    pre_act = jnp.dot(second_low, expand_full, preferred_element_type=f32) + expand_vec.astype(f32)
    hidden, gelu_back = jax.vjp(exact_gelu, pre_act)
    hidden_low = hidden.astype(low_type)
    reduced = jnp.dot(hidden_low, reduce_full, preferred_element_type=f32) + reduce_vec.astype(f32)
    result = ((resid + reduced) * live_rows).astype(low_type)
    expand_back = expand_full
    reduce_back = reduce_full
    upstream_live = upstream.astype(f32) * live_rows
    out_low = upstream_live.astype(low_type)
    reduce_grad = jnp.einsum("rf,rd->fd", hidden_low, out_low, preferred_element_type=f32)
    reducebias_grad = column_sums(out_low)
    hidden_grad = jnp.einsum("rd,fd->rf", out_low, reduce_back, preferred_element_type=f32)
    (pre_grad,) = gelu_back(hidden_grad)
    pre_low = pre_grad.astype(low_type)
    expand_grad = jnp.einsum("rd,rf->df", second_low, pre_low, preferred_element_type=f32)
    expandbias_grad = column_sums(pre_low)
    second_grad = jnp.einsum("rf,df->rd", pre_low, expand_back, preferred_element_type=f32)
    resid_part, gaintwo_grad, shifttwo_grad = second_back(second_grad)
    resid_grad = upstream_live + resid_part
    feed_sums = (
        lax.psum_scatter(
            gaintwo_grad.astype(jnp.bfloat16), "grp", scatter_dimension=0, tiled=True
        ).astype(jnp.float32),
        lax.psum_scatter(
            shifttwo_grad.astype(jnp.bfloat16), "grp", scatter_dimension=0, tiled=True
        ).astype(jnp.float32),
        lax.psum_scatter(
            expand_grad.astype(jnp.bfloat16), "grp", scatter_dimension=0, tiled=True
        ).astype(jnp.float32),
        lax.psum_scatter(
            expandbias_grad.astype(jnp.bfloat16), "grp", scatter_dimension=0, tiled=True
        ).astype(jnp.float32),
        lax.psum_scatter(
            reduce_grad.astype(jnp.bfloat16), "grp", scatter_dimension=0, tiled=True
        ).astype(jnp.float32),
        lax.psum_scatter(
            reducebias_grad.astype(jnp.bfloat16), "grp", scatter_dimension=0, tiled=True
        ).astype(jnp.float32),
    )
    feed_owned = (
        lax.psum(feed_sums[0].astype(jnp.bfloat16), "rep").astype(jnp.float32),
        lax.psum(feed_sums[1].astype(jnp.bfloat16), "rep").astype(jnp.float32),
        lax.psum(feed_sums[2].astype(jnp.bfloat16), "rep").astype(jnp.float32),
        lax.psum(feed_sums[3].astype(jnp.bfloat16), "rep").astype(jnp.float32),
        lax.psum(feed_sums[4].astype(jnp.bfloat16), "rep").astype(jnp.float32),
        lax.psum(feed_sums[5].astype(jnp.bfloat16), "rep").astype(jnp.float32),
    )
    triple_back = triple_full
    merge_back = merge_full
    branch_low = resid_grad.astype(low_type)
    merge_grad = jnp.einsum("ra,rd->ad", attended, branch_low, preferred_element_type=f32)
    mergebias_grad = column_sums(branch_low)
    att_grad = jnp.einsum("rd,ad->ra", branch_low, merge_back, preferred_element_type=f32)
    att_low = att_grad.astype(low_type).reshape(groups, slots, heads, head_size)
    again_weights = jnp.exp(make_scores() - log_total)
    value_grad = jnp.einsum(
        "ghqk,gqhd->gkhd", again_weights.astype(low_type), att_low, preferred_element_type=f32
    )
    weight_grad = jnp.einsum("gqhd,gkhd->ghqk", att_low, values, preferred_element_type=f32)
    inner = jnp.sum(again_weights * weight_grad, axis=-1, keepdims=True)
    score_low = (again_weights * (weight_grad - inner) * scale).astype(low_type)
    query_grad = jnp.einsum("ghqk,gkhd->gqhd", score_low, keys, preferred_element_type=f32)
    key_grad = jnp.einsum("ghqk,gqhd->gkhd", score_low, query, preferred_element_type=f32)
    triple_low = jnp.concatenate(
        [
            query_grad.reshape(rows, width),
            key_grad.reshape(rows, width),
            value_grad.reshape(rows, width),
        ],
        axis=1,
    ).astype(low_type)
    triple_grad = jnp.einsum("rd,re->de", normed_low, triple_low, preferred_element_type=f32)
    triplebias_grad = jnp.concatenate(
        [column_sums(triple_low[:, :width]), column_sums(triple_low[:, 2 * width :])]
    )
    normed_grad = jnp.einsum("re,de->rd", triple_low, triple_back, preferred_element_type=f32)
    token_part, gainone_grad, shiftone_grad = first_back(normed_grad)
    tokens_grad = (resid_grad + token_part).astype(low_type)
    attend_sums = (
        lax.psum_scatter(
            gainone_grad.astype(jnp.bfloat16), "grp", scatter_dimension=0, tiled=True
        ).astype(jnp.float32),
        lax.psum_scatter(
            shiftone_grad.astype(jnp.bfloat16), "grp", scatter_dimension=0, tiled=True
        ).astype(jnp.float32),
        lax.psum_scatter(
            triple_grad.astype(jnp.bfloat16), "grp", scatter_dimension=0, tiled=True
        ).astype(jnp.float32),
        lax.psum_scatter(
            triplebias_grad.astype(jnp.bfloat16), "grp", scatter_dimension=0, tiled=True
        ).astype(jnp.float32),
        lax.psum_scatter(
            merge_grad.astype(jnp.bfloat16), "grp", scatter_dimension=0, tiled=True
        ).astype(jnp.float32),
        lax.psum_scatter(
            mergebias_grad.astype(jnp.bfloat16), "grp", scatter_dimension=0, tiled=True
        ).astype(jnp.float32),
    )
    attend_owned = (
        lax.psum(attend_sums[0].astype(jnp.bfloat16), "rep").astype(jnp.float32),
        lax.psum(attend_sums[1].astype(jnp.bfloat16), "rep").astype(jnp.float32),
        lax.psum(attend_sums[2].astype(jnp.bfloat16), "rep").astype(jnp.float32),
        lax.psum(attend_sums[3].astype(jnp.bfloat16), "rep").astype(jnp.float32),
        lax.psum(attend_sums[4].astype(jnp.bfloat16), "rep").astype(jnp.float32),
        lax.psum(attend_sums[5].astype(jnp.bfloat16), "rep").astype(jnp.float32),
    )
    return (
        result,
        tokens_grad,
        attend_owned[0],
        attend_owned[1],
        attend_owned[2],
        attend_owned[3],
        attend_owned[4],
        attend_owned[5],
        feed_owned[0],
        feed_owned[1],
        feed_owned[2],
        feed_owned[3],
        feed_owned[4],
        feed_owned[5],
    )


def fits(mesh):
    return mesh.shape["rep"] == 8 and mesh.shape["grp"] == 4


def solution(mesh):
    return jax.shard_map(
        fast_device if fits(mesh) else per_device,
        mesh=mesh,
        in_specs=(
            P(("rep", "grp"), None),
            P(("rep", "grp")),
            P("grp"),
            P("grp"),
            P("grp", None),
            P("grp"),
            P("grp", None),
            P("grp"),
            P("grp"),
            P("grp"),
            P("grp", None),
            P("grp"),
            P("grp", None),
            P("grp"),
            P(("rep", "grp"), None),
        ),
        out_specs=(
            P(("rep", "grp"), None),
            P(("rep", "grp"), None),
            P("grp"),
            P("grp"),
            P("grp", None),
            P("grp"),
            P("grp", None),
            P("grp"),
            P("grp"),
            P("grp"),
            P("grp", None),
            P("grp"),
            P("grp", None),
            P("grp"),
        ),
        check_vma=False,
    )
```
